32 devices in a mesh: blk: 8 (over y, x, core), wide: 4 (over z).
Axes of the slice: x: 2, y: 2, z: 4, core: 2. Of those that a mesh axis runs over, the one named last changes fastest.
Arguments:
- coupling: bfloat16 [1024, 8, 2, 512], P('blk', 'wide'), may hold values from -0.09375 to 0.09375
- rp_cells: int32 [3, 1024], replicated, may hold values from -8 to 7
- re_cells: int32 [3, 8], P(None, 'wide'), may hold values from -8 to 7
- q_points: int32 [3, 2048], P(None, 'blk'), may hold values from 0 to 31
- k_points: int32 [3, 2], replicated, may hold values from 0 to 31
- mode_energy: float32 [16, 2048], P(None, 'blk'), may hold values from 0.02 to 1
Outputs:
- bloch_coupling: float32 [2, 2, 512, 2048], P(None, None, 'wide', 'blk')
The draws below stay inside these ranges and needn't reach their ends.
All inputs are finite; a program needn't handle non-finite values.
Results may differ from the reference program's by a relative error of at most 0.002.
Values may be sent and summed in bfloat16 or wider, within the bound.
No kernel may reach another device: no remote copies, remote signals or barrier semaphores. Data moves between devices by JAX's collectives and lax.ppermute only.
A program may use at most 64 MiB of HBM per device.

```python
import math
import jax
import jax.numpy as jnp
from jax import lax

RP = 1024
MODES = 16
K = 2
MESHQ = 32
MESHK = 32
E = 512
Q = 2048
RE = 8


def place_ends(drawn, key, smallest, largest):
    extent = drawn.shape
    spot = [jax.random.randint(jax.random.fold_in(key, axis), (), 0, extent[axis]) for axis in range(len(extent))]
    drawn = drawn.at[tuple(spot)].set(smallest)
    longest = extent.index(max(extent))
    spot[longest] = (spot[longest] + 1) % extent[longest]
    return drawn.at[tuple(spot)].set(largest)


def with_spikes(values, rng, source, target, shards_of, factor):
    def block_of(position):
        return (jnp.arange(values.shape[position]) // (values.shape[position] // shards_of)).reshape((-1,) + (1,) * (values.ndim - 1 - position))

    first = jax.random.permutation(rng, shards_of)[block_of(target)]
    far = (block_of(target) + shards_of // 2) % shards_of
    return jnp.where((block_of(source) == first) | (block_of(source) == far), factor * values, values)


def block_scale(own_key, shape, cuts, low, high):
    level = 1.0
    for position, shards_of in cuts:
        steps = jax.random.uniform(jax.random.fold_in(jax.random.fold_in(own_key, 6), position), (shards_of,), jnp.float32, low / len(cuts), high / len(cuts))
        level = level * jnp.repeat(jnp.exp(steps), shape[position] // shards_of).reshape((-1,) + (1,) * (len(shape) - 1 - position))
    return level


def gaussian_with(key, shape, scale, reach, pieces, heavy, held_as=jnp.bfloat16):
    entries = scale * jax.random.normal(key, shape, jnp.float32)
    if pieces:
        entries = entries * block_scale(key, shape, pieces, -0.22, 0.18)
    return jnp.clip(with_spikes(entries, jax.random.fold_in(key, 3), *heavy), -reach, reach).astype(held_as)


def setup_inputs(seed: int = 0) -> dict:
    splits = jax.random.split(jax.random.key(seed), 7)
    coupling = gaussian_with(splits[0], (RP, RE, 2, E), (RP * RE) ** -0.5, 0.09375, ((0, 8), (1, 4)), (1, 3, 4, 2.0))
    rp_cells = place_ends(jax.random.randint(splits[1], (3, RP), -8, 8), jax.random.fold_in(splits[1], 1), -8, 7).astype(jnp.int32)
    re_cells = place_ends(jax.random.randint(splits[2], (3, RE), -8, 8), jax.random.fold_in(splits[2], 1), -8, 7).astype(jnp.int32)
    q_points = place_ends(jax.random.randint(splits[3], (3, Q), 0, MESHQ), jax.random.fold_in(splits[3], 1), 0, MESHQ - 1).astype(jnp.int32)
    k_points = place_ends(jax.random.randint(splits[4], (3, K), 0, MESHK), jax.random.fold_in(splits[4], 1), 0, MESHK - 1).astype(jnp.int32)
    mode_energy = jnp.clip(jnp.exp(math.log(1.0) - 3.912023 * jax.random.uniform(splits[5], (MODES, Q), jnp.float32) ** block_scale(splits[5], (MODES, Q), ((1, 8),), -0.2, 0.2)), 0.02, 1.0)
    return {"coupling": coupling, "rp_cells": rp_cells, "re_cells": re_cells, "q_points": q_points, "k_points": k_points, "mode_energy": mode_energy}


def phase_parts(left, right, modulus):
    whole = lax.optimization_barrier(jnp.sum(left[:, :, None] * right[:, None, :], axis=0))
    angle = jnp.mod(whole, modulus).astype(jnp.float32) * (2.0 * math.pi / modulus)
    return (jnp.cos(angle), jnp.sin(angle))

def reference(coupling, rp_cells, re_cells, q_points, k_points, mode_energy):
    cosine, sine = phase_parts(q_points, rp_cells, MESHQ)
    cosine = cosine.astype(jnp.bfloat16)
    sine = sine.astype(jnp.bfloat16)
    k_cos, k_sin = phase_parts(k_points, re_cells, MESHK)
    weight = 1.0 / jnp.sqrt(2.0 * mode_energy)
    entry_weight = weight[jnp.arange(E, dtype=jnp.int32) % MODES]

    def one_cell(total, index):
        slab = lax.dynamic_index_in_dim(coupling, index, 1, keepdims=False)
        flat = slab.reshape(RP, 2 * E)
        with_cos = lax.dot_general(flat, cosine, (((0,), (1,)), ((), ())), preferred_element_type=jnp.float32)
        with_sin = lax.dot_general(flat, sine, (((0,), (1,)), ((), ())), preferred_element_type=jnp.float32)
        real = (with_cos[:E] - with_sin[E:]) * entry_weight
        imag = (with_cos[E:] + with_sin[:E]) * entry_weight
        cos_one = lax.dynamic_index_in_dim(k_cos, index, 1, keepdims=False)[:, None, None]
        sin_one = lax.dynamic_index_in_dim(k_sin, index, 1, keepdims=False)[:, None, None]
        part_re = cos_one * real[None] - sin_one * imag[None]
        part_im = cos_one * imag[None] + sin_one * real[None]
        return (total + jnp.stack([part_re, part_im], axis=1), None)
    start = jnp.zeros((K, 2, E, Q), jnp.float32)
    total, _ = lax.scan(one_cell, start, jnp.arange(RE, dtype=jnp.int32))
    return total
```

```python
import functools
import math

import jax
import jax.numpy as jnp
from jax import lax
from jax.experimental import pallas as pl
from jax.experimental.pallas import tpu as pltpu
from jax.sharding import PartitionSpec as P

MODES = 16
MESHQ = 32
MESHK = 32
LANES = 128
TAIL = 4
SHARES = (1,)


def xor_pairs(count, step):
    return [(i, i ^ step) for i in range(count)]


def swap(value, axis, count, step):
    return lax.ppermute(value, axis, xor_pairs(count, step))


def slice_kernel(starts, steps, entries, x_ref, tail_ref, *rest):
    outs, sem = rest[:-1], rest[-1]
    me = lax.axis_index("wide")
    copies = []
    for c, (first, rows) in enumerate(starts):
        for j, step in enumerate(steps):
            out = outs[c * len(steps) + j]
            column = pl.multiple_of((me ^ step) * entries, LANES)
            copies.append(
                pltpu.make_async_copy(
                    x_ref.at[pl.ds(first, rows), :, :, pl.ds(column, entries)],
                    out.at[pl.ds(0, rows)],
                    sem.at[2 * len(copies)],
                )
            )
    tails = []
    for i, out in enumerate(outs):
        rows = starts[i // len(steps)][1]
        tails.append(
            pltpu.make_async_copy(tail_ref, out.at[pl.ds(rows, TAIL)], sem.at[2 * i + 1])
        )
    for copy in copies + tails:
        copy.start()
    for copy in copies + tails:
        copy.wait()


def cut(coupling, tail, starts, steps, entries):
    cells = coupling.shape[1]
    shapes = []
    for _, rows in starts:
        for _ in steps:
            shapes.append(
                jax.ShapeDtypeStruct((rows + TAIL, cells, 2, entries), coupling.dtype)
            )
    return pl.pallas_call(
        functools.partial(slice_kernel, starts, steps, entries),
        out_shape=shapes,
        in_specs=[pl.BlockSpec(memory_space=pl.ANY)] * 2,
        out_specs=[pl.BlockSpec(memory_space=pl.ANY)] * len(shapes),
        scratch_shapes=[pltpu.SemaphoreType.DMA((2 * len(shapes),))],
        name="cut",
    )(coupling, tail)


def combine_kernel(rows, cells, entries, waves, *refs):
    ins = refs[: -2]
    out, work = refs[-2], refs[-1]
    per = 2 * cells
    phases = []
    for i, ref in enumerate(ins):
        work[i] = ref[...].astype(jnp.float32)
    for i in range(len(ins)):
        angle = work[i, pl.ds(rows * per, 8), :] * (2.0 * math.pi / MESHK)
        phases.append((jnp.cos(angle), jnp.sin(angle)))
    step = 32
    for first in range(0, rows, step):
        re = [None] * waves
        im = [None] * waves
        for i in range(len(ins)):
            cos, sin = phases[i]
            for r in range(cells):
                a = work[i, pl.ds(first * per + 2 * r, step, stride=per), :]
                b = work[i, pl.ds(first * per + 2 * r + 1, step, stride=per), :]
                for k in range(waves):
                    at = r * waves + k
                    c = cos[at : at + 1, :]
                    s = sin[at : at + 1, :]
                    x = c * a - s * b
                    y = c * b + s * a
                    re[k] = x if re[k] is None else re[k] + x
                    im[k] = y if im[k] is None else im[k] + y
        for k in range(waves):
            lanes = pl.ds(k * entries, entries)
            out[pl.ds(first, step), lanes] = re[k].astype(out.dtype)
            out[pl.ds(rows + first, step), lanes] = im[k].astype(out.dtype)


def combine(blocks, rows, cells, entries, waves):
    flat = [b.reshape(b.shape[0] * 2 * cells, entries) for b in blocks]
    full = flat[0].shape[0]
    return pl.pallas_call(
        functools.partial(combine_kernel, rows, cells, entries, waves),
        out_shape=jax.ShapeDtypeStruct((2 * rows, waves * entries), jnp.bfloat16),
        in_specs=[pl.BlockSpec(memory_space=pltpu.VMEM)] * len(flat),
        out_specs=pl.BlockSpec(memory_space=pltpu.VMEM),
        scratch_shapes=[pltpu.VMEM((len(flat), full, entries), jnp.float32)],
        name="combine",
    )(*flat)


def table_kernel(starts, slab, rp_ref, q_ref, out_ref):
    lane = lax.broadcasted_iota(jnp.int32, (8, LANES), 1) % MESHQ
    angle = lane.astype(jnp.float32) * (2.0 * math.pi / MESHQ)
    cos_table = jnp.cos(angle)
    sin_table = jnp.sin(angle)
    blocks = out_ref.shape[0]
    q_local = q_ref.shape[1]
    step = 32

    for block in range(blocks):
        row = 0
        for first, rows in starts:
            n = lax.dot_general(
                rp_ref[:, pl.ds(block * slab, slab)],
                q_ref[...],
                (((0,), (0,)), ((), ())),
                preferred_element_type=jnp.float32,
            )
            m = n - MESHQ * jnp.floor(n * (1.0 / MESHQ))
            index = m.astype(jnp.int32)
            for top in range(first, first + rows, step):
                for left in range(0, q_local, LANES):
                    cos_rows = []
                    sin_rows = []
                    for sub in range(0, step, 8):
                        at = index[top + sub : top + sub + 8, left : left + LANES]
                        cos_rows.append(
                            jnp.take_along_axis(
                                cos_table, at, axis=1, mode="promise_in_bounds"
                            )
                        )
                        sin_rows.append(
                            jnp.take_along_axis(
                                sin_table, at, axis=1, mode="promise_in_bounds"
                            )
                        )
                    c = jnp.concatenate(cos_rows, axis=0)
                    s = jnp.concatenate(sin_rows, axis=0)
                    re_rows = pl.ds(row + top - first, step)
                    im_rows = pl.ds(row + rows + top - first, step)
                    near = pl.ds(left, LANES)
                    far = pl.ds(q_local + left, LANES)
                    cb = c.astype(jnp.bfloat16)
                    sb = s.astype(jnp.bfloat16)
                    nb = (-s).astype(jnp.bfloat16)
                    out_ref[block, re_rows, near] = cb
                    out_ref[block, re_rows, far] = sb
                    out_ref[block, im_rows, near] = nb
                    out_ref[block, im_rows, far] = cb
            row += 2 * rows


def table(rp_cells, q_points, starts, slab):
    blocks = rp_cells.shape[1] // slab
    q_local = q_points.shape[1]
    pad = ((0, 16 - rp_cells.shape[0]), (0, 0))
    rp = jnp.pad(rp_cells.astype(jnp.bfloat16), pad)
    q = jnp.pad(q_points.astype(jnp.bfloat16), pad)
    return pl.pallas_call(
        functools.partial(table_kernel, starts, slab),
        out_shape=jax.ShapeDtypeStruct((blocks, 2 * slab, 2 * q_local), jnp.bfloat16),
        in_specs=[pl.BlockSpec(memory_space=pltpu.VMEM)] * 2,
        out_specs=pl.BlockSpec(memory_space=pltpu.VMEM),
        cost_estimate=pl.CostEstimate(
            flops=8 * blocks * slab * q_local * 10,
            bytes_accessed=blocks * slab * q_local * 8,
            transcendentals=0,
        ),
        name="table",
    )(rp, q)


def product_kernel(pieces, waves, entries, table_ref, energy_ref, *refs):
    ins, out, acc = refs[: len(pieces)], refs[-2], refs[-1]
    me = lax.axis_index("blk")
    q_local = energy_ref.shape[1]
    for i, (step, row, rows) in enumerate(pieces):
        part = lax.dot_general(
            ins[i][...],
            table_ref[me ^ step, pl.ds(row, rows), :],
            (((0,), (0,)), ((), ())),
            preferred_element_type=jnp.float32,
        )
        if i == 0:
            acc[...] = part
        else:
            acc[...] += part
    weight = 1.0 / jnp.sqrt(2.0 * energy_ref[...])
    for k in range(waves):
        for part in range(2):
            for e in range(0, entries, MODES):
                out[k, part, pl.ds(e, MODES), :] = (
                    acc[pl.ds(k * entries + e, MODES), pl.ds(part * q_local, q_local)]
                    * weight
                )


def product(tables, energy, blocks, pieces, waves, entries):
    q_local = energy.shape[1]
    return pl.pallas_call(
        functools.partial(product_kernel, pieces, waves, entries),
        out_shape=jax.ShapeDtypeStruct((waves, 2, entries, q_local), jnp.float32),
        in_specs=[pl.BlockSpec(memory_space=pltpu.VMEM)] * (2 + len(blocks)),
        out_specs=pl.BlockSpec(memory_space=pltpu.VMEM),
        scratch_shapes=[pltpu.VMEM((waves * entries, 2 * q_local), jnp.float32)],
        name="product",
    )(tables, energy, *blocks)


def direct(blk, wide, coupling, rp_cells, re_cells, q_points, k_points, mode_energy):
    slab, cells, _, total = coupling.shape
    entries = total // wide
    waves = k_points.shape[1]
    unit = slab // sum(SHARES)
    starts = []
    for share in SHARES:
        starts.append((sum(r for _, r in starts), share * unit))

    turn = jnp.mod(
        jnp.sum(re_cells[:, :, None] * k_points[:, None, :], axis=0), MESHK
    )
    tail = jnp.broadcast_to(
        turn.astype(coupling.dtype)[None, :, :, None], (TAIL, cells, waves, entries)
    )
    steps = tuple(range(wide - 1, -1, -1))
    cuts = cut(coupling, tail, starts, steps, entries)
    tables = table(rp_cells, q_points, starts, slab)

    moved = []
    for i, block in enumerate(cuts):
        step = steps[i % len(steps)]
        moved.append(swap(block, "wide", wide, step) if step else block)
    blocks, pieces = [], []
    row = 0
    for c, (_, rows) in enumerate(starts):
        group = moved[c * len(steps) : (c + 1) * len(steps)]
        mine = combine(group, rows, cells, entries, waves)
        held = {0: mine}
        for step in range(blk - 2, 0, -2):
            held[step] = swap(mine, "blk", blk, step)
        for step in list(held):
            held[step + 1] = swap(held[step], "blk", blk, 1)
        for step, value in held.items():
            blocks.append(value)
            pieces.append((step, row, 2 * rows))
        row += 2 * rows
    return product(tables, mode_energy, blocks, pieces, waves, entries)


def phase_parts(left, right, modulus):
    whole = jnp.sum(left[:, :, None] * right[:, None, :], axis=0)
    angle = jnp.mod(whole, modulus).astype(jnp.float32) * (2.0 * math.pi / modulus)
    return (jnp.cos(angle), jnp.sin(angle))


def general(coupling, rp_cells, re_cells, q_points, k_points, mode_energy):
    moved = lax.all_to_all(coupling, "wide", split_axis=3, concat_axis=1, tiled=True)
    cells = lax.all_gather(re_cells, "wide", axis=1, tiled=True)
    entries = moved.shape[3]
    offset = lax.axis_index("wide") * entries
    k_cos, k_sin = phase_parts(k_points, cells, MESHK)
    real = moved[:, :, 0].astype(jnp.float32)
    imag = moved[:, :, 1].astype(jnp.float32)
    high = lax.Precision.HIGHEST
    turn = functools.partial(jnp.einsum, "kr,pre->pke", precision=high)
    held = jnp.stack(
        [turn(k_cos, real) - turn(k_sin, imag), turn(k_cos, imag) + turn(k_sin, real)],
        axis=2,
    ).astype(coupling.dtype)
    full = lax.all_gather(held, "blk", axis=0, tiled=True)
    cosine, sine = phase_parts(q_points, rp_cells, MESHQ)
    dot = functools.partial(
        jnp.einsum, "qp,pkse->skeq", preferred_element_type=jnp.float32
    )
    with_cos = dot(cosine.astype(full.dtype), full)
    with_sin = dot(sine.astype(full.dtype), full)
    index = (offset + jnp.arange(entries, dtype=jnp.int32)) % MODES
    weight = (1.0 / jnp.sqrt(2.0 * mode_energy))[index]
    return jnp.stack(
        [(with_cos[0] - with_sin[1]) * weight, (with_cos[1] + with_sin[0]) * weight],
        axis=1,
    )


def solution(mesh):
    blk, wide = mesh.shape["blk"], mesh.shape["wide"]

    def on_device(coupling, rp_cells, re_cells, q_points, k_points, mode_energy):
        args = (coupling, rp_cells, re_cells, q_points, k_points, mode_energy)
        slab, cells, _, total = coupling.shape
        waves = k_points.shape[1]
        fits = (
            blk & (blk - 1) == 0
            and wide & (wide - 1) == 0
            and blk > 1
            and total // wide == LANES
            and cells == 2
            and waves == 2
            and slab % 128 == 0
            and q_points.shape[1] % LANES == 0
        )
        return direct(blk, wide, *args) if fits else general(*args)

    in_specs = (
        P("blk", "wide", None, None),
        P(),
        P(None, "wide"),
        P(None, "blk"),
        P(),
        P(None, "blk"),
    )
    out_specs = P(None, None, "wide", "blk")
    return jax.shard_map(
        on_device, mesh=mesh, in_specs=in_specs, out_specs=out_specs, check_vma=False
    )
```

```python
import functools
import math

import jax
import jax.numpy as jnp
from jax import lax
from jax.experimental import pallas as pl
from jax.experimental.pallas import tpu as pltpu
from jax.sharding import PartitionSpec as P


MODES = 16
MESHQ = 32
MESHK = 32
LANES = 128
TAIL = 4
SHARES = (1,)
LATE = 2


def xor_pairs(count, step):
    return [(i, i ^ step) for i in range(count)]


def swap(value, axis, count, step):
    return lax.ppermute(value, axis, xor_pairs(count, step))


def grant(mebibytes):
    return pltpu.CompilerParams(vmem_limit_bytes=int(mebibytes * 2**20))


def cut_kernel(starts, steps, entries, x_ref, cells_ref, points_ref, *rest):
    outs = rest[:-4]
    cells, points, sem, small = rest[-4:]
    me = lax.axis_index("wide")
    copies = [
        pltpu.make_async_copy(cells_ref, cells, small.at[0]),
        pltpu.make_async_copy(points_ref, points, small.at[1]),
    ]
    for c, (first, rows) in enumerate(starts):
        for j, step in enumerate(steps):
            i = c * len(steps) + j
            column = pl.multiple_of((me ^ step) * entries, LANES)
            copies.append(
                pltpu.make_async_copy(
                    x_ref.at[pl.ds(first, rows), :, :, pl.ds(column, entries)],
                    outs[i].at[pl.ds(0, rows)],
                    sem.at[i],
                )
            )
    for copy in copies:
        copy.start()
    for copy in copies[:2]:
        copy.wait()
    shape = (TAIL,) + outs[0].shape[1:]
    which_cell = lax.broadcasted_iota(jnp.int32, shape, 1)
    which_wave = lax.broadcasted_iota(jnp.int32, shape, 2)
    tail = jnp.zeros(shape, jnp.float32)
    for r in range(cells.shape[0]):
        for k in range(points.shape[0]):
            turn = cells[r, 0] * points[k, 0]
            for axis in range(1, cells.shape[1]):
                turn += cells[r, axis] * points[k, axis]
            turn = lax.rem(lax.rem(turn, MESHK) + MESHK, MESHK)
            here = (which_cell == r) & (which_wave == k)
            tail = jnp.where(here, turn.astype(jnp.float32), tail)
    tail = tail.astype(outs[0].dtype)
    for i, out in enumerate(outs):
        rows = starts[i // len(steps)][1]
        out[pl.ds(rows, TAIL)] = tail
    for copy in copies[2:]:
        copy.wait()


def cut(coupling, re_cells, k_points, starts, steps, entries):
    cells = coupling.shape[1]
    shapes = []
    for _, rows in starts:
        for _ in steps:
            shapes.append(
                jax.ShapeDtypeStruct((rows + TAIL, cells, 2, entries), coupling.dtype)
            )
    return pl.pallas_call(
        functools.partial(cut_kernel, starts, steps, entries),
        out_shape=shapes,
        in_specs=[pl.BlockSpec(memory_space=pl.ANY)] * 3,
        out_specs=[pl.BlockSpec(memory_space=pltpu.VMEM)] * len(shapes),
        scratch_shapes=[
            pltpu.SMEM(re_cells.shape[::-1], jnp.int32),
            pltpu.SMEM(k_points.shape[::-1], jnp.int32),
            pltpu.SemaphoreType.DMA((len(shapes),)),
            pltpu.SemaphoreType.DMA((2,)),
        ],
        compiler_params=grant(4),
        name="cut",
    )(coupling, re_cells.T, k_points.T)


def circle(modulus):
    lane = lax.broadcasted_iota(jnp.int32, (8, LANES), 1) % modulus
    angle = lane.astype(jnp.float32) * (2.0 * math.pi / modulus)
    return jnp.cos(angle), jnp.sin(angle)


def look(values, index):
    return jnp.take_along_axis(values, index, axis=1, mode="promise_in_bounds")


def combine_kernel(rows, cells, entries, waves, cos_ref, sin_ref, *refs):
    ins = refs[:-2]
    out, work = refs[-2], refs[-1]
    per = 2 * cells
    phases = []
    for i, ref in enumerate(ins):
        work[i] = ref[...].astype(jnp.float32)
    for i in range(len(ins)):
        turn = work[i, pl.ds(rows * per, 8), :].astype(jnp.int32)
        phases.append((look(cos_ref[...], turn), look(sin_ref[...], turn)))
    step = 32
    for first in range(0, rows, step):
        re = [None] * waves
        im = [None] * waves
        for i in range(len(ins)):
            cos, sin = phases[i]
            for r in range(cells):
                a = work[i, pl.ds(first * per + 2 * r, step, stride=per), :]
                b = work[i, pl.ds(first * per + 2 * r + 1, step, stride=per), :]
                for k in range(waves):
                    at = r * waves + k
                    c = cos[at : at + 1, :]
                    s = sin[at : at + 1, :]
                    x = c * a - s * b
                    y = c * b + s * a
                    re[k] = x if re[k] is None else re[k] + x
                    im[k] = y if im[k] is None else im[k] + y
        for k in range(waves):
            lanes = pl.ds(k * entries, entries)
            out[pl.ds(first, step), lanes] = re[k].astype(out.dtype)
            out[pl.ds(rows + first, step), lanes] = im[k].astype(out.dtype)


def combine(circles, blocks, rows, cells, entries, waves):
    flat = [b.reshape(b.shape[0] * 2 * cells, entries) for b in blocks]
    full = flat[0].shape[0]
    return pl.pallas_call(
        functools.partial(combine_kernel, rows, cells, entries, waves),
        out_shape=jax.ShapeDtypeStruct((2 * rows, waves * entries), jnp.bfloat16),
        in_specs=[pl.BlockSpec(memory_space=pltpu.VMEM)] * (2 + len(flat)),
        out_specs=pl.BlockSpec(memory_space=pltpu.VMEM),
        scratch_shapes=[pltpu.VMEM((len(flat), full, entries), jnp.float32)],
        compiler_params=grant(6),
        name="combine",
    )(*circles, *flat)


def table_kernel(starts, slab, rp_ref, q_ref, out_ref, cos_ref, sin_ref):
    cos_ref[...], sin_ref[...] = circle(MESHK)
    cos_table, sin_table = circle(MESHQ)
    blocks = out_ref.shape[0]
    q_local = q_ref.shape[1]
    step = 32
    q = q_ref[...].astype(jnp.bfloat16)
    for block in range(blocks):
        n = lax.dot_general(
            rp_ref[:, pl.ds(block * slab, slab)].astype(jnp.bfloat16),
            q,
            (((0,), (0,)), ((), ())),
            preferred_element_type=jnp.float32,
        )
        m = n - MESHQ * jnp.floor(n * (1.0 / MESHQ))
        index = m.astype(jnp.int32)
        row = 0
        for first, rows in starts:
            for top in range(first, first + rows, step):
                for left in range(0, q_local, LANES):
                    cos_rows = []
                    sin_rows = []
                    for sub in range(top, top + step, 8):
                        at = index[sub : sub + 8, left : left + LANES]
                        cos_rows.append(look(cos_table, at))
                        sin_rows.append(look(sin_table, at))
                    c = jnp.concatenate(cos_rows, axis=0).astype(jnp.bfloat16)
                    s = jnp.concatenate(sin_rows, axis=0).astype(jnp.bfloat16)
                    re_rows = pl.ds(row + top - first, step)
                    im_rows = pl.ds(row + rows + top - first, step)
                    near = pl.ds(left, LANES)
                    far = pl.ds(q_local + left, LANES)
                    out_ref[block, re_rows, near] = c
                    out_ref[block, re_rows, far] = s
                    out_ref[block, im_rows, near] = -s
                    out_ref[block, im_rows, far] = c
            row += 2 * rows


def table(rp_cells, q_points, starts, slab):
    blocks = rp_cells.shape[1] // slab
    q_local = q_points.shape[1]
    spot = jax.ShapeDtypeStruct((8, LANES), jnp.float32)
    return pl.pallas_call(
        functools.partial(table_kernel, starts, slab),
        out_shape=[
            jax.ShapeDtypeStruct((blocks, 2 * slab, 2 * q_local), jnp.bfloat16),
            spot,
            spot,
        ],
        in_specs=[pl.BlockSpec(memory_space=pltpu.VMEM)] * 2,
        out_specs=[pl.BlockSpec(memory_space=pltpu.VMEM)] * 3,
        compiler_params=grant(6),
        cost_estimate=pl.CostEstimate(
            flops=8 * blocks * slab * q_local * 10,
            bytes_accessed=blocks * slab * q_local * 8,
            transcendentals=0,
        ),
        name="table",
    )(rp_cells, q_points)


def partial_kernel(pieces, table_ref, *refs):
    ins, out = refs[:-1], refs[-1]
    me = lax.axis_index("blk")
    for i, (step, row, rows) in enumerate(pieces):
        part = lax.dot_general(
            ins[i][...],
            table_ref[me ^ step, pl.ds(row, rows), :],
            (((0,), (0,)), ((), ())),
            preferred_element_type=jnp.float32,
        )
        if i == 0:
            out[...] = part
        else:
            out[...] += part


def partial(tables, blocks, pieces):
    shape = (blocks[0].shape[1], tables.shape[2])
    depth = sum(piece[2] for piece in pieces)
    return pl.pallas_call(
        functools.partial(partial_kernel, pieces),
        out_shape=jax.ShapeDtypeStruct(shape, jnp.float32),
        in_specs=[pl.BlockSpec(memory_space=pltpu.VMEM)] * (1 + len(blocks)),
        out_specs=pl.BlockSpec(memory_space=pltpu.VMEM),
        compiler_params=grant(8),
        cost_estimate=pl.CostEstimate(
            flops=2 * depth * shape[0] * shape[1],
            bytes_accessed=4 * shape[0] * shape[1],
            transcendentals=0,
        ),
        name="partial",
    )(tables, *blocks)


def finish_kernel(pieces, waves, entries, table_ref, energy_ref, sum_ref, *refs):
    ins, out, held, sem = refs[:-3], refs[-3], refs[-2], refs[-1]
    me = lax.axis_index("blk")
    q_local = energy_ref.shape[1]
    weight = 1.0 / jnp.sqrt(2.0 * energy_ref[...])
    copies = []
    for k in range(waves):
        lanes = pl.ds(k * entries, entries)
        total = sum_ref[lanes, :]
        for i, (step, row, rows) in enumerate(pieces):
            total += lax.dot_general(
                ins[i][:, lanes],
                table_ref[me ^ step, pl.ds(row, rows), :],
                (((0,), (0,)), ((), ())),
                preferred_element_type=jnp.float32,
            )
        for part in range(2):
            for e in range(0, entries, MODES):
                held[k, part, pl.ds(e, MODES), :] = (
                    total[e : e + MODES, part * q_local : (part + 1) * q_local] * weight
                )
        copies.append(pltpu.make_async_copy(held.at[k], out.at[k], sem.at[k]))
        copies[-1].start()
    for copy in copies:
        copy.wait()


def finish(tables, energy, total, blocks, pieces, waves, entries):
    q_local = energy.shape[1]
    shape = (waves, 2, entries, q_local)
    return pl.pallas_call(
        functools.partial(finish_kernel, pieces, waves, entries),
        out_shape=jax.ShapeDtypeStruct(shape, jnp.float32),
        in_specs=[pl.BlockSpec(memory_space=pltpu.VMEM)] * (3 + len(blocks)),
        out_specs=pl.BlockSpec(memory_space=pl.ANY),
        scratch_shapes=[
            pltpu.VMEM(shape, jnp.float32),
            pltpu.SemaphoreType.DMA((waves,)),
        ],
        compiler_params=grant(8),
        name="finish",
    )(tables, energy, total, *blocks)


def direct(blk, wide, coupling, rp_cells, re_cells, q_points, k_points, mode_energy):
    slab, cells, _, total = coupling.shape
    entries = total // wide
    waves = k_points.shape[1]
    unit = slab // sum(SHARES)
    starts = []
    for share in SHARES:
        starts.append((sum(r for _, r in starts), share * unit))

    steps = tuple(range(wide - 1, -1, -1))
    cuts = cut(coupling, re_cells, k_points, starts, steps, entries)
    tables, *circles = table(rp_cells, q_points, starts, slab)

    moved = []
    for i, block in enumerate(cuts):
        step = steps[i % len(steps)]
        moved.append(swap(block, "wide", wide, step) if step else block)
    early, late = [], []
    row = 0
    for c, (_, rows) in enumerate(starts):
        group = moved[c * len(steps) : (c + 1) * len(steps)]
        mine = combine(circles, group, rows, cells, entries, waves)
        held = {0: mine}
        for step in range(blk - 2, 0, -2):
            held[step] = swap(mine, "blk", blk, step)
        for step in list(held):
            held[step + 1] = swap(held[step], "blk", blk, 1)
        for step, value in held.items():
            final = c == len(starts) - 1 and step >= LATE
            (late if final else early).append((value, (step, row, 2 * rows)))
        row += 2 * rows
    total = partial(tables, [v for v, _ in early], [p for _, p in early])
    return finish(
        tables,
        mode_energy,
        total,
        [v for v, _ in late],
        [p for _, p in late],
        waves,
        entries,
    )


def phase_parts(left, right, modulus):
    whole = jnp.sum(left[:, :, None] * right[:, None, :], axis=0)
    angle = jnp.mod(whole, modulus).astype(jnp.float32) * (2.0 * math.pi / modulus)
    return (jnp.cos(angle), jnp.sin(angle))


def general(coupling, rp_cells, re_cells, q_points, k_points, mode_energy):
    moved = lax.all_to_all(coupling, "wide", split_axis=3, concat_axis=1, tiled=True)
    cells = lax.all_gather(re_cells, "wide", axis=1, tiled=True)
    entries = moved.shape[3]
    offset = lax.axis_index("wide") * entries
    k_cos, k_sin = phase_parts(k_points, cells, MESHK)
    real = moved[:, :, 0].astype(jnp.float32)
    imag = moved[:, :, 1].astype(jnp.float32)
    high = lax.Precision.HIGHEST
    turn = functools.partial(jnp.einsum, "kr,pre->pke", precision=high)
    held = jnp.stack(
        [turn(k_cos, real) - turn(k_sin, imag), turn(k_cos, imag) + turn(k_sin, real)],
        axis=2,
    ).astype(coupling.dtype)
    full = lax.all_gather(held, "blk", axis=0, tiled=True)
    cosine, sine = phase_parts(q_points, rp_cells, MESHQ)
    dot = functools.partial(
        jnp.einsum, "qp,pkse->skeq", preferred_element_type=jnp.float32
    )
    with_cos = dot(cosine.astype(full.dtype), full)
    with_sin = dot(sine.astype(full.dtype), full)
    index = (offset + jnp.arange(entries, dtype=jnp.int32)) % MODES
    weight = (1.0 / jnp.sqrt(2.0 * mode_energy))[index]
    return jnp.stack(
        [(with_cos[0] - with_sin[1]) * weight, (with_cos[1] + with_sin[0]) * weight],
        axis=1,
    )


def solution(mesh):
    blk, wide = mesh.shape["blk"], mesh.shape["wide"]

    def on_device(coupling, rp_cells, re_cells, q_points, k_points, mode_energy):
        args = (coupling, rp_cells, re_cells, q_points, k_points, mode_energy)
        slab, cells, _, total = coupling.shape
        waves = k_points.shape[1]
        fits = (
            blk & (blk - 1) == 0
            and wide & (wide - 1) == 0
            and blk > 1
            and total // wide == LANES
            and cells == 2
            and waves == 2
            and slab % 128 == 0
            and q_points.shape[1] % LANES == 0
        )
        if not fits:
            return general(*args)
        return direct(blk, wide, *args)

    in_specs = (
        P("blk", "wide", None, None),
        P(),
        P(None, "wide"),
        P(None, "blk"),
        P(),
        P(None, "blk"),
    )
    out_specs = P(None, None, "wide", "blk")
    return jax.shard_map(
        on_device, mesh=mesh, in_specs=in_specs, out_specs=out_specs, check_vma=False
    )
```

```python
import functools
import math

import jax
import jax.numpy as jnp
from jax import lax
from jax.experimental import pallas as pl
from jax.experimental.pallas import tpu as pltpu
from jax.sharding import PartitionSpec as P


MODES = 16
MESHQ = 32
MESHK = 32
LANES = 128
TAIL = 4
SHARES = (1,)
GROUPS = (0, 0, 1, 2, 0, 1, 1, 2)
ROUNDS = "x123"


def xor_pairs(count, step):
    return [(i, i ^ step) for i in range(count)]


def rounds(count):
    xor = {i: xor_pairs(count, i) for i in range(1, count)}
    up = [(i, i + 1) for i in range(count - 1)]
    down = [(j, i) for i, j in up]
    middle = [(1, 2), (2, 1)]
    ends = [(0, 3), (3, 0)]
    return {
        "x123": (xor[1], xor[2], xor[3]),
        "x213": (xor[2], xor[1], xor[3]),
        "ud23": (up, down, xor[2], xor[3]),
        "ud32": (up, down, xor[3], xor[2]),
        "u2d3": (up, xor[2], down, xor[3]),
        "m213": (middle, xor[2], xor[1], ends),
        "m231": (middle, xor[2], ends, xor[1]),
        "m123": (middle, xor[1], xor[2], ends),
        "2ud3": (xor[2], up, down, ends),
        "2m13": (xor[2], middle, xor[1], ends),
        "2m31": (xor[2], middle, ends, xor[1]),
    }[ROUNDS]


def swap(value, axis, count, step):
    return lax.ppermute(value, axis, xor_pairs(count, step))


def grant(mebibytes):
    return pltpu.CompilerParams(vmem_limit_bytes=int(mebibytes * 2**20))


def cut_kernel(starts, steps, entries, x_ref, cells_ref, points_ref, *rest):
    outs = rest[:-4]
    cells, points, sem, small = rest[-4:]
    me = lax.axis_index("wide")
    copies = [
        pltpu.make_async_copy(cells_ref, cells, small.at[0]),
        pltpu.make_async_copy(points_ref, points, small.at[1]),
    ]
    for c, (first, rows) in enumerate(starts):
        for j, step in enumerate(steps):
            i = c * len(steps) + j
            target = sum(jnp.where(me == one, two, 0) for one, two in step)
            column = pl.multiple_of(target * entries, LANES)
            copies.append(
                pltpu.make_async_copy(
                    x_ref.at[pl.ds(first, rows), :, :, pl.ds(column, entries)],
                    outs[i].at[pl.ds(0, rows)],
                    sem.at[i],
                )
            )
    for copy in copies:
        copy.start()
    for copy in copies[:2]:
        copy.wait()
    shape = (TAIL,) + outs[0].shape[1:]
    which_cell = lax.broadcasted_iota(jnp.int32, shape, 1)
    which_wave = lax.broadcasted_iota(jnp.int32, shape, 2)
    tail = jnp.zeros(shape, jnp.float32)
    for r in range(cells.shape[0]):
        for k in range(points.shape[0]):
            turn = cells[r, 0] * points[k, 0]
            for axis in range(1, cells.shape[1]):
                turn += cells[r, axis] * points[k, axis]
            turn = lax.rem(lax.rem(turn, MESHK) + MESHK, MESHK)
            here = (which_cell == r) & (which_wave == k)
            tail = jnp.where(here, turn.astype(jnp.float32), tail)
    tail = tail.astype(outs[0].dtype)
    for i, out in enumerate(outs):
        rows = starts[i // len(steps)][1]
        out[pl.ds(rows, TAIL)] = tail
    for copy in copies[2:]:
        copy.wait()


def stay(array):
    return pltpu.with_memory_space_constraint(array, pltpu.HBM)


def cut(coupling, re_cells, k_points, starts, steps, entries):
    cells = coupling.shape[1]
    shapes = []
    for _, rows in starts:
        for _ in steps:
            shapes.append(
                jax.ShapeDtypeStruct((rows + TAIL, cells, 2, entries), coupling.dtype)
            )
    return pl.pallas_call(
        functools.partial(cut_kernel, starts, steps, entries),
        out_shape=shapes,
        in_specs=[pl.BlockSpec(memory_space=pltpu.HBM)] * 3,
        out_specs=[pl.BlockSpec(memory_space=pltpu.VMEM)] * len(shapes),
        scratch_shapes=[
            pltpu.SMEM(re_cells.shape[::-1], jnp.int32),
            pltpu.SMEM(k_points.shape[::-1], jnp.int32),
            pltpu.SemaphoreType.DMA((len(shapes),)),
            pltpu.SemaphoreType.DMA((2,)),
        ],
        compiler_params=grant(2),
        name="cut",
    )(*[stay(x) for x in (coupling, re_cells.T, k_points.T)])


def circle(modulus):
    lane = lax.broadcasted_iota(jnp.int32, (8, LANES), 1) % modulus
    angle = lane.astype(jnp.float32) * (2.0 * math.pi / modulus)
    return jnp.cos(angle), jnp.sin(angle)


def look(values, index):
    return jnp.take_along_axis(values, index, axis=1, mode="promise_in_bounds")


def combine_kernel(rows, cells, entries, waves, cos_ref, sin_ref, *refs):
    ins = refs[:-2]
    out, work = refs[-2], refs[-1]
    per = 2 * cells
    phases = []
    for i, ref in enumerate(ins):
        work[i] = ref[...].astype(jnp.float32)
    for i in range(len(ins)):
        turn = work[i, pl.ds(rows * per, 8), :].astype(jnp.int32)
        phases.append((look(cos_ref[...], turn), look(sin_ref[...], turn)))
    step = 32
    for first in range(0, rows, step):
        re = [None] * waves
        im = [None] * waves
        for i in range(len(ins)):
            cos, sin = phases[i]
            for r in range(cells):
                a = work[i, pl.ds(first * per + 2 * r, step, stride=per), :]
                b = work[i, pl.ds(first * per + 2 * r + 1, step, stride=per), :]
                for k in range(waves):
                    at = r * waves + k
                    c = cos[at : at + 1, :]
                    s = sin[at : at + 1, :]
                    x = c * a - s * b
                    y = c * b + s * a
                    re[k] = x if re[k] is None else re[k] + x
                    im[k] = y if im[k] is None else im[k] + y
        for k in range(waves):
            lanes = pl.ds(k * entries, entries)
            out[pl.ds(first, step), lanes] = re[k].astype(out.dtype)
            out[pl.ds(rows + first, step), lanes] = im[k].astype(out.dtype)


def combine(circles, blocks, rows, cells, entries, waves):
    flat = [b.reshape(b.shape[0] * 2 * cells, entries) for b in blocks]
    full = flat[0].shape[0]
    return pl.pallas_call(
        functools.partial(combine_kernel, rows, cells, entries, waves),
        out_shape=jax.ShapeDtypeStruct((2 * rows, waves * entries), jnp.bfloat16),
        in_specs=[pl.BlockSpec(memory_space=pltpu.VMEM)] * (2 + len(flat)),
        out_specs=pl.BlockSpec(memory_space=pltpu.VMEM),
        scratch_shapes=[pltpu.VMEM((len(flat), full, entries), jnp.float32)],
        compiler_params=grant(6),
        name="combine",
    )(*circles, *flat)


def table_kernel(starts, slab, rp_ref, q_ref, out_ref, cos_ref, sin_ref):
    cos_ref[...], sin_ref[...] = circle(MESHK)
    cos_table, sin_table = circle(MESHQ)
    blocks = out_ref.shape[0]
    q_local = q_ref.shape[1]
    step = 32
    q = q_ref[...].astype(jnp.bfloat16)
    for block in range(blocks):
        n = lax.dot_general(
            rp_ref[:, pl.ds(block * slab, slab)].astype(jnp.bfloat16),
            q,
            (((0,), (0,)), ((), ())),
            preferred_element_type=jnp.float32,
        )
        m = n - MESHQ * jnp.floor(n * (1.0 / MESHQ))
        index = m.astype(jnp.int32)
        row = 0
        for first, rows in starts:
            for top in range(first, first + rows, step):
                for left in range(0, q_local, LANES):
                    cos_rows = []
                    sin_rows = []
                    for sub in range(top, top + step, 8):
                        at = index[sub : sub + 8, left : left + LANES]
                        cos_rows.append(look(cos_table, at))
                        sin_rows.append(look(sin_table, at))
                    c = jnp.concatenate(cos_rows, axis=0).astype(jnp.bfloat16)
                    s = jnp.concatenate(sin_rows, axis=0).astype(jnp.bfloat16)
                    re_rows = pl.ds(row + top - first, step)
                    im_rows = pl.ds(row + rows + top - first, step)
                    near = pl.ds(left, LANES)
                    far = pl.ds(q_local + left, LANES)
                    out_ref[block, re_rows, near] = c
                    out_ref[block, re_rows, far] = s
                    out_ref[block, im_rows, near] = -s
                    out_ref[block, im_rows, far] = c
            row += 2 * rows


def table(rp_cells, q_points, starts, slab):
    blocks = rp_cells.shape[1] // slab
    q_local = q_points.shape[1]
    spot = jax.ShapeDtypeStruct((8, LANES), jnp.float32)
    return pl.pallas_call(
        functools.partial(table_kernel, starts, slab),
        out_shape=[
            jax.ShapeDtypeStruct((blocks, 2 * slab, 2 * q_local), jnp.bfloat16),
            spot,
            spot,
        ],
        in_specs=[pl.BlockSpec(memory_space=pltpu.VMEM)] * 2,
        out_specs=[pl.BlockSpec(memory_space=pltpu.VMEM)] * 3,
        compiler_params=grant(6),
        cost_estimate=pl.CostEstimate(
            flops=8 * blocks * slab * q_local * 10,
            bytes_accessed=blocks * slab * q_local * 8,
            transcendentals=0,
        ),
        name="table",
    )(rp_cells, q_points)


def partial_kernel(pieces, more, table_ref, *refs):
    ins, out = refs[:-1], refs[-1]
    me = lax.axis_index("blk")
    total = ins[-1][...] if more else None
    for i, (step, row, rows) in enumerate(pieces):
        part = lax.dot_general(
            ins[i][...],
            table_ref[me ^ step, pl.ds(row, rows), :],
            (((0,), (0,)), ((), ())),
            preferred_element_type=jnp.float32,
        )
        total = part if total is None else total + part
    out[...] = total


def partial(tables, held, total):
    blocks = [value for value, _ in held]
    pieces = [piece for _, piece in held]
    shape = (blocks[0].shape[1], tables.shape[2])
    depth = sum(piece[2] for piece in pieces)
    more = [] if total is None else [total]
    return pl.pallas_call(
        functools.partial(partial_kernel, pieces, bool(more)),
        out_shape=jax.ShapeDtypeStruct(shape, jnp.float32),
        in_specs=[pl.BlockSpec(memory_space=pltpu.VMEM)] * (1 + len(blocks) + len(more)),
        out_specs=pl.BlockSpec(memory_space=pltpu.VMEM),
        compiler_params=grant(8),
        cost_estimate=pl.CostEstimate(
            flops=2 * depth * shape[0] * shape[1],
            bytes_accessed=4 * shape[0] * shape[1],
            transcendentals=0,
        ),
        name="partial",
    )(tables, *blocks, *more)


def finish_kernel(pieces, waves, entries, table_ref, energy_ref, sum_ref, *refs):
    ins, out, held, sem = refs[:-3], refs[-3], refs[-2], refs[-1]
    me = lax.axis_index("blk")
    q_local = energy_ref.shape[1]
    weight = 1.0 / jnp.sqrt(2.0 * energy_ref[...])
    copies = []
    for k in range(waves):
        lanes = pl.ds(k * entries, entries)
        total = sum_ref[lanes, :]
        for i, (step, row, rows) in enumerate(pieces):
            total += lax.dot_general(
                ins[i][:, lanes],
                table_ref[me ^ step, pl.ds(row, rows), :],
                (((0,), (0,)), ((), ())),
                preferred_element_type=jnp.float32,
            )
        for part in range(2):
            for e in range(0, entries, MODES):
                held[k, part, pl.ds(e, MODES), :] = (
                    total[e : e + MODES, part * q_local : (part + 1) * q_local] * weight
                )
        copies.append(pltpu.make_async_copy(held.at[k], out.at[k], sem.at[k]))
        copies[-1].start()
    for copy in copies:
        copy.wait()


def finish(tables, energy, total, blocks, pieces, waves, entries):
    q_local = energy.shape[1]
    shape = (waves, 2, entries, q_local)
    return pl.pallas_call(
        functools.partial(finish_kernel, pieces, waves, entries),
        out_shape=jax.ShapeDtypeStruct(shape, jnp.float32),
        in_specs=[pl.BlockSpec(memory_space=pltpu.VMEM)] * (3 + len(blocks)),
        out_specs=pl.BlockSpec(memory_space=pl.ANY),
        scratch_shapes=[
            pltpu.VMEM(shape, jnp.float32),
            pltpu.SemaphoreType.DMA((waves,)),
        ],
        compiler_params=grant(8),
        name="finish",
    )(tables, energy, total, *blocks)


def direct(blk, wide, coupling, rp_cells, re_cells, q_points, k_points, mode_energy):
    slab, cells, _, total = coupling.shape
    entries = total // wide
    waves = k_points.shape[1]
    unit = slab // sum(SHARES)
    starts = []
    for share in SHARES:
        starts.append((sum(r for _, r in starts), share * unit))

    steps = rounds(wide)
    home = [(i, i) for i in range(wide)]
    cuts = cut(coupling, re_cells, k_points, starts, steps, entries)
    kept = cut(coupling, re_cells, k_points, starts, (home,), entries)
    tables, *circles = table(rp_cells, q_points, starts, slab)

    moved = []
    for i, block in enumerate(cuts):
        c, step = divmod(i, len(steps))
        moved.append(lax.ppermute(block, "wide", steps[step]))
    groups = {}
    row = 0
    for c, (_, rows) in enumerate(starts):
        group = [kept[c]] + moved[c * len(steps) : (c + 1) * len(steps)]
        mine = combine(circles, group, rows, cells, entries, waves)
        held = {0: mine}
        for step in range(blk - 2, 0, -2):
            held[step] = swap(mine, "blk", blk, step)
        for step in list(held):
            held[step + 1] = swap(held[step], "blk", blk, 1)
        for step, value in held.items():
            name = GROUPS[step] if c == len(starts) - 1 else 0
            groups.setdefault((c, name), []).append((value, (step, row, 2 * rows)))
        row += 2 * rows
    total = None
    names = sorted(groups)
    for c, name in names[:-1]:
        total = partial(tables, groups[c, name], total)
    return finish(
        tables,
        mode_energy,
        total,
        [v for v, _ in groups[names[-1]]],
        [p for _, p in groups[names[-1]]],
        waves,
        entries,
    )


def phase_parts(left, right, modulus):
    whole = jnp.sum(left[:, :, None] * right[:, None, :], axis=0)
    angle = jnp.mod(whole, modulus).astype(jnp.float32) * (2.0 * math.pi / modulus)
    return (jnp.cos(angle), jnp.sin(angle))


def general(coupling, rp_cells, re_cells, q_points, k_points, mode_energy):
    moved = lax.all_to_all(coupling, "wide", split_axis=3, concat_axis=1, tiled=True)
    cells = lax.all_gather(re_cells, "wide", axis=1, tiled=True)
    entries = moved.shape[3]
    offset = lax.axis_index("wide") * entries
    k_cos, k_sin = phase_parts(k_points, cells, MESHK)
    real = moved[:, :, 0].astype(jnp.float32)
    imag = moved[:, :, 1].astype(jnp.float32)
    high = lax.Precision.HIGHEST
    turn = functools.partial(jnp.einsum, "kr,pre->pke", precision=high)
    held = jnp.stack(
        [turn(k_cos, real) - turn(k_sin, imag), turn(k_cos, imag) + turn(k_sin, real)],
        axis=2,
    ).astype(coupling.dtype)
    full = lax.all_gather(held, "blk", axis=0, tiled=True)
    cosine, sine = phase_parts(q_points, rp_cells, MESHQ)
    dot = functools.partial(
        jnp.einsum, "qp,pkse->skeq", preferred_element_type=jnp.float32
    )
    with_cos = dot(cosine.astype(full.dtype), full)
    with_sin = dot(sine.astype(full.dtype), full)
    index = (offset + jnp.arange(entries, dtype=jnp.int32)) % MODES
    weight = (1.0 / jnp.sqrt(2.0 * mode_energy))[index]
    return jnp.stack(
        [(with_cos[0] - with_sin[1]) * weight, (with_cos[1] + with_sin[0]) * weight],
        axis=1,
    )


def solution(mesh):
    blk, wide = mesh.shape["blk"], mesh.shape["wide"]

    def on_device(coupling, rp_cells, re_cells, q_points, k_points, mode_energy):
        args = (coupling, rp_cells, re_cells, q_points, k_points, mode_energy)
        slab, cells, _, total = coupling.shape
        waves = k_points.shape[1]
        fits = (
            blk & (blk - 1) == 0
            and wide & (wide - 1) == 0
            and blk > 1
            and total // wide == LANES
            and cells == 2
            and wide == 4
            and waves == 2
            and slab % 128 == 0
            and q_points.shape[1] % LANES == 0
        )
        if not fits:
            return general(*args)
        return direct(blk, wide, *args)

    in_specs = (
        P("blk", "wide", None, None),
        P(),
        P(None, "wide"),
        P(None, "blk"),
        P(),
        P(None, "blk"),
    )
    out_specs = P(None, None, "wide", "blk")
    return jax.shard_map(
        on_device, mesh=mesh, in_specs=in_specs, out_specs=out_specs, check_vma=False
    )
```

```python
import functools
import math

import jax
import jax.numpy as jnp
from jax import lax
from jax.experimental import pallas as pl
from jax.experimental.pallas import tpu as pltpu
from jax.sharding import PartitionSpec as P


MODES = 16
MESHQ = 32
MESHK = 32
LANES = 128
TAIL = 4
NEAR = (4, 6, 2)
LAST = 96
ORDER = ("pair", "two", "three", "one", "sum")
EARLY = 1
CODED = 1
BITS = 14.0


def xor_pairs(count, step):
    return [(i, i ^ step) for i in range(count)]


def swap(value, axis, count, step):
    return lax.ppermute(value, axis, xor_pairs(count, step))


def grant(mebibytes):
    return pltpu.CompilerParams(vmem_limit_bytes=int(mebibytes * 2**20))


def cut_kernel(parts, rings, more, entries, x_ref, cells_ref, points_ref, *rest):
    extra, rest = rest[:more], rest[more:]
    outs = rest[: len(parts)]
    cells, points, sem, small = rest[-4:]
    me = lax.axis_index("wide")
    copies = [
        pltpu.make_async_copy(cells_ref, cells, small.at[0]),
        pltpu.make_async_copy(points_ref, points, small.at[1]),
    ]
    for i, (step, first, rows) in enumerate(parts):
        column = pl.multiple_of((me ^ step) * entries, LANES)
        copies.append(
            pltpu.make_async_copy(
                x_ref.at[pl.ds(first, rows), :, :, pl.ds(column, entries)],
                outs[i].at[pl.ds(0, rows)],
                sem.at[i],
            )
        )
    for i in range(more):
        out = rest[len(parts) + 2 * rings + i]
        copies.append(pltpu.make_async_copy(extra[i], out, small.at[2 + i]))
    for copy in copies:
        copy.start()
    if rings:
        rest[len(parts)][...], rest[len(parts) + 1][...] = circle(MESHK)
    for copy in copies[:2]:
        copy.wait()
    shape = (TAIL,) + outs[0].shape[1:]
    which_cell = lax.broadcasted_iota(jnp.int32, shape, 1)
    which_wave = lax.broadcasted_iota(jnp.int32, shape, 2)
    tail = jnp.zeros(shape, jnp.float32)
    for r in range(cells.shape[0]):
        for k in range(points.shape[0]):
            turn = cells[r, 0] * points[k, 0]
            for axis in range(1, cells.shape[1]):
                turn += cells[r, axis] * points[k, axis]
            turn = lax.rem(lax.rem(turn, MESHK) + MESHK, MESHK)
            here = (which_cell == r) & (which_wave == k)
            tail = jnp.where(here, turn.astype(jnp.float32), tail)
    tail = tail.astype(outs[0].dtype)
    for (_, _, rows), out in zip(parts, outs):
        out[pl.ds(rows, TAIL)] = tail
    for copy in copies[2:]:
        copy.wait()


def stay(array):
    return pltpu.with_memory_space_constraint(array, pltpu.HBM)


def cut(coupling, re_cells, k_points, parts, rings, extra, entries):
    cells = coupling.shape[1]
    shapes = [
        jax.ShapeDtypeStruct((rows + TAIL, cells, 2, entries), coupling.dtype)
        for _, _, rows in parts
    ]
    count = len(shapes)
    shapes += [jax.ShapeDtypeStruct((8, LANES), jnp.float32)] * (2 * rings)
    shapes += [jax.ShapeDtypeStruct(array.shape, array.dtype) for array in extra]
    arrays = (coupling, re_cells.T, k_points.T) + tuple(extra)
    outs = pl.pallas_call(
        functools.partial(cut_kernel, parts, rings, len(extra), entries),
        out_shape=shapes,
        in_specs=[pl.BlockSpec(memory_space=pltpu.HBM)] * len(arrays),
        out_specs=[pl.BlockSpec(memory_space=pltpu.VMEM)] * len(shapes),
        scratch_shapes=[
            pltpu.SMEM(re_cells.shape[::-1], jnp.int32),
            pltpu.SMEM(k_points.shape[::-1], jnp.int32),
            pltpu.SemaphoreType.DMA((count,)),
            pltpu.SemaphoreType.DMA((2 + len(extra),)),
        ],
        compiler_params=grant(2),
        name="cut",
    )(*[stay(array) for array in arrays])
    return outs[:count], outs[count:]


def circle(modulus):
    lane = lax.broadcasted_iota(jnp.int32, (8, LANES), 1) % modulus
    angle = lane.astype(jnp.float32) * (2.0 * math.pi / modulus)
    return jnp.cos(angle), jnp.sin(angle)


def look(values, index):
    return jnp.take_along_axis(values, index, axis=1, mode="promise_in_bounds")


def combine_kernel(spans, rows, cells, waves, adds, cos_ref, sin_ref, *refs):
    count = len(spans)
    ins, plus = refs[:count], refs[count : count + len(adds)]
    out, work, sums = refs[-3:]
    entries = work.shape[2]
    coded = out.dtype == jnp.int16
    target = sums if coded else out
    per = 2 * cells
    phases = []
    for i, ref in enumerate(ins):
        work[i, pl.ds(0, ref.shape[0]), :] = ref[...].astype(jnp.float32)
    for i, (_, size) in enumerate(spans):
        turn = work[i, pl.ds(size * per, 8), :].astype(jnp.int32)
        phases.append((look(cos_ref[...], turn), look(sin_ref[...], turn)))
    step = 32
    for first in range(0, rows, step):
        re = [None] * waves
        im = [None] * waves
        for (begin, size), ref in zip(adds, plus):
            if not begin <= first < begin + size:
                continue
            for k in range(waves):
                lanes = pl.ds(k * entries, entries)
                x = ref[pl.ds(first - begin, step), lanes].astype(jnp.float32)
                y = ref[pl.ds(size + first - begin, step), lanes].astype(jnp.float32)
                if ref.dtype == jnp.int16:
                    power = ref[pl.ds(2 * size, 16), lanes].astype(jnp.float32)
                    unit = jnp.exp2(power[0:1, :] - BITS)
                    x, y = x * unit, y * unit
                re[k] = x if re[k] is None else re[k] + x
                im[k] = y if im[k] is None else im[k] + y
        for i, (begin, size) in enumerate(spans):
            if not begin <= first < begin + size:
                continue
            cos, sin = phases[i]
            for r in range(cells):
                start = (first - begin) * per + 2 * r
                a = work[i, pl.ds(start, step, stride=per), :]
                b = work[i, pl.ds(start + 1, step, stride=per), :]
                for k in range(waves):
                    at = r * waves + k
                    c = cos[at : at + 1, :]
                    s = sin[at : at + 1, :]
                    x = c * a - s * b
                    y = c * b + s * a
                    re[k] = x if re[k] is None else re[k] + x
                    im[k] = y if im[k] is None else im[k] + y
        for k in range(waves):
            lanes = pl.ds(k * entries, entries)
            target[pl.ds(first, step), lanes] = re[k].astype(target.dtype)
            target[pl.ds(rows + first, step), lanes] = im[k].astype(target.dtype)
    if coded:
        value = sums[...]
        top = jnp.max(jnp.abs(value), axis=0, keepdims=True)
        power = jnp.ceil(jnp.log2(jnp.maximum(top, 2.0**-100)))
        scaled = jnp.round(value * jnp.exp2(BITS - power)).astype(jnp.int32)
        out[pl.ds(0, 2 * rows), :] = scaled.astype(jnp.int16)
        spread = jnp.broadcast_to(power, (16, value.shape[1])).astype(jnp.int32)
        out[pl.ds(2 * rows, 16), :] = spread.astype(jnp.int16)


def combine(circles, blocks, spans, plus, adds, rows, waves, dtype):
    cells, _, entries = blocks[0].shape[1:]
    flat = [b.reshape(b.shape[0] * 2 * cells, entries) for b in blocks]
    full = max(b.shape[0] for b in flat)
    coded = dtype == jnp.int16
    shape = (2 * rows, waves * entries)
    tall = (2 * rows + 16 * coded, waves * entries)
    return pl.pallas_call(
        functools.partial(combine_kernel, spans, rows, cells, waves, adds),
        out_shape=jax.ShapeDtypeStruct(tall, dtype),
        in_specs=[pl.BlockSpec(memory_space=pltpu.VMEM)] * (2 + len(flat) + len(plus)),
        out_specs=pl.BlockSpec(memory_space=pltpu.VMEM),
        scratch_shapes=[
            pltpu.VMEM((len(flat), full, entries), jnp.float32),
            pltpu.VMEM(shape if coded else (8, LANES), jnp.float32),
        ],
        compiler_params=grant(6),
        name="combine",
    )(*circles, *flat, *plus)


def table_kernel(slab, rp_ref, q_ref, out_ref):
    cos_table, sin_table = circle(MESHQ)
    blocks = out_ref.shape[0]
    q_local = q_ref.shape[1]
    step = 32
    q = q_ref[...].astype(jnp.bfloat16)
    for block in range(blocks):
        n = lax.dot_general(
            rp_ref[:, pl.ds(block * slab, slab)].astype(jnp.bfloat16),
            q,
            (((0,), (0,)), ((), ())),
            preferred_element_type=jnp.float32,
        )
        m = n - MESHQ * jnp.floor(n * (1.0 / MESHQ))
        index = m.astype(jnp.int32)
        for top in range(0, slab, step):
            for left in range(0, q_local, LANES):
                cos_rows = []
                sin_rows = []
                for sub in range(top, top + step, 8):
                    at = index[sub : sub + 8, left : left + LANES]
                    cos_rows.append(look(cos_table, at))
                    sin_rows.append(look(sin_table, at))
                c = jnp.concatenate(cos_rows, axis=0).astype(jnp.bfloat16)
                s = jnp.concatenate(sin_rows, axis=0).astype(jnp.bfloat16)
                near = pl.ds(left, LANES)
                far = pl.ds(q_local + left, LANES)
                out_ref[block, pl.ds(top, step), near] = c
                out_ref[block, pl.ds(top, step), far] = s
                out_ref[block, pl.ds(slab + top, step), near] = -s
                out_ref[block, pl.ds(slab + top, step), far] = c


def table(rp_cells, q_points, slab):
    blocks = rp_cells.shape[1] // slab
    q_local = q_points.shape[1]
    shape = (blocks, 2 * slab, 2 * q_local)
    return pl.pallas_call(
        functools.partial(table_kernel, slab),
        out_shape=jax.ShapeDtypeStruct(shape, jnp.bfloat16),
        in_specs=[pl.BlockSpec(memory_space=pltpu.VMEM)] * 2,
        out_specs=pl.BlockSpec(memory_space=pltpu.VMEM),
        compiler_params=grant(6),
        cost_estimate=pl.CostEstimate(
            flops=8 * blocks * slab * q_local * 10,
            bytes_accessed=blocks * slab * q_local * 8,
            transcendentals=0,
        ),
        name="table",
    )(rp_cells, q_points)


def partial_kernel(pieces, more, table_ref, *refs):
    ins, out = refs[:-1], refs[-1]
    me = lax.axis_index("blk")
    total = ins[-1][...] if more else None
    for i, step in enumerate(pieces):
        part = lax.dot_general(
            ins[i][...],
            table_ref[me ^ step],
            (((0,), (0,)), ((), ())),
            preferred_element_type=jnp.float32,
        )
        total = part if total is None else total + part
    out[...] = total


def partial(tables, held, total):
    blocks = [value for value, _ in held]
    pieces = [piece for _, piece in held]
    shape = (blocks[0].shape[1], tables.shape[2])
    depth = len(pieces) * tables.shape[1]
    more = [] if total is None else [total]
    return pl.pallas_call(
        functools.partial(partial_kernel, pieces, bool(more)),
        out_shape=jax.ShapeDtypeStruct(shape, jnp.float32),
        in_specs=[pl.BlockSpec(memory_space=pltpu.VMEM)] * (1 + len(blocks) + len(more)),
        out_specs=pl.BlockSpec(memory_space=pltpu.VMEM),
        compiler_params=grant(8),
        cost_estimate=pl.CostEstimate(
            flops=2 * depth * shape[0] * shape[1],
            bytes_accessed=4 * shape[0] * shape[1],
            transcendentals=0,
        ),
        name="partial",
    )(tables, *blocks, *more)


def finish_kernel(pieces, waves, entries, table_ref, energy_ref, sum_ref, *refs):
    ins, out, held, sem = refs[:-3], refs[-3], refs[-2], refs[-1]
    me = lax.axis_index("blk")
    q_local = energy_ref.shape[1]
    weight = 1.0 / jnp.sqrt(2.0 * energy_ref[...])
    copies = []
    for k in range(waves):
        lanes = pl.ds(k * entries, entries)
        total = sum_ref[lanes, :]
        for i, step in enumerate(pieces):
            total += lax.dot_general(
                ins[i][:, lanes],
                table_ref[me ^ step],
                (((0,), (0,)), ((), ())),
                preferred_element_type=jnp.float32,
            )
        for part in range(2):
            for e in range(0, entries, MODES):
                held[k, part, pl.ds(e, MODES), :] = (
                    total[e : e + MODES, part * q_local : (part + 1) * q_local] * weight
                )
        copies.append(pltpu.make_async_copy(held.at[k], out.at[k], sem.at[k]))
        copies[-1].start()
    for copy in copies:
        copy.wait()


def finish(tables, energy, total, blocks, pieces, waves, entries):
    q_local = energy.shape[1]
    shape = (waves, 2, entries, q_local)
    return pl.pallas_call(
        functools.partial(finish_kernel, pieces, waves, entries),
        out_shape=jax.ShapeDtypeStruct(shape, jnp.float32),
        in_specs=[pl.BlockSpec(memory_space=pltpu.VMEM)] * (3 + len(blocks)),
        out_specs=pl.BlockSpec(memory_space=pl.ANY),
        scratch_shapes=[
            pltpu.VMEM(shape, jnp.float32),
            pltpu.SemaphoreType.DMA((waves,)),
        ],
        compiler_params=grant(8),
        name="finish",
    )(tables, energy, total, *blocks)


def direct(blk, wide, coupling, rp_cells, re_cells, q_points, k_points, mode_energy):
    slab, _, _, total = coupling.shape
    entries = total // wide
    waves = k_points.shape[1]
    most = slab - LAST
    rest = (most, LAST)

    sent = {"one": (1, 0, slab), "two": (2, 0, most), "three": (3, 0, most)}
    if LAST:
        sent["pair"] = (3, most, LAST)
    if not most:
        del sent["two"], sent["three"]
    names = [name for name in ORDER if name in sent]
    parts = [sent[name] for name in names] + [(2, most, LAST)] * bool(LAST)
    arrays = (coupling, re_cells, k_points)
    cuts, circles = cut(*arrays, parts, True, [], entries)
    mid = list(cuts[len(names) :])
    extra = (rp_cells, q_points)
    (own,), extra = cut(*arrays, [(0, 0, slab)], False, extra, entries)
    tables = table(*extra, slab)

    got = {}
    for name, block in zip(names, cuts):
        got[name] = swap(block, "wide", wide, 1 if name == "pair" else sent[name][0])
    plus, adds = [], []
    if LAST:
        dtype = jnp.int16 if CODED else jnp.bfloat16
        both = combine(
            circles, mid + [got["pair"]], [(0, LAST)] * 2, [], [], LAST, waves, dtype
        )
        plus.append(swap(both, "wide", wide, 2))
        adds.append(rest)
    blocks, spans = [own, got["one"]], [(0, slab)] * 2
    if EARLY:
        some = combine(circles, blocks, spans, [], [], slab, waves, jnp.float32)
        plus.append(some)
        adds.append((0, slab))
        blocks, spans = [], []
    if most:
        blocks += [got["two"], got["three"]]
        spans += [(0, most)] * 2
    mine = combine(circles, blocks, spans, plus, adds, slab, waves, jnp.bfloat16)

    held = {0: mine}
    for step in range(blk - 2, 0, -2):
        held[step] = swap(mine, "blk", blk, step)
    for step in list(held):
        held[step + 1] = swap(held[step], "blk", blk, 1)
    first, second, third = NEAR
    groups = [
        (0, 1, first),
        (third, first + 1, second),
        (third + 1, second + 1),
    ]
    total = None
    for steps in groups[:-1]:
        total = partial(tables, [(held[step], step) for step in steps], total)
    return finish(
        tables,
        mode_energy,
        total,
        [held[step] for step in groups[-1]],
        groups[-1],
        waves,
        entries,
    )


def phase_parts(left, right, modulus):
    whole = jnp.sum(left[:, :, None] * right[:, None, :], axis=0)
    angle = jnp.mod(whole, modulus).astype(jnp.float32) * (2.0 * math.pi / modulus)
    return (jnp.cos(angle), jnp.sin(angle))


def general(coupling, rp_cells, re_cells, q_points, k_points, mode_energy):
    moved = lax.all_to_all(coupling, "wide", split_axis=3, concat_axis=1, tiled=True)
    cells = lax.all_gather(re_cells, "wide", axis=1, tiled=True)
    entries = moved.shape[3]
    offset = lax.axis_index("wide") * entries
    k_cos, k_sin = phase_parts(k_points, cells, MESHK)
    real = moved[:, :, 0].astype(jnp.float32)
    imag = moved[:, :, 1].astype(jnp.float32)
    high = lax.Precision.HIGHEST
    turn = functools.partial(jnp.einsum, "kr,pre->pke", precision=high)
    held = jnp.stack(
        [turn(k_cos, real) - turn(k_sin, imag), turn(k_cos, imag) + turn(k_sin, real)],
        axis=2,
    ).astype(coupling.dtype)
    full = lax.all_gather(held, "blk", axis=0, tiled=True)
    cosine, sine = phase_parts(q_points, rp_cells, MESHQ)
    dot = functools.partial(
        jnp.einsum, "qp,pkse->skeq", preferred_element_type=jnp.float32
    )
    with_cos = dot(cosine.astype(full.dtype), full)
    with_sin = dot(sine.astype(full.dtype), full)
    index = (offset + jnp.arange(entries, dtype=jnp.int32)) % MODES
    weight = (1.0 / jnp.sqrt(2.0 * mode_energy))[index]
    return jnp.stack(
        [(with_cos[0] - with_sin[1]) * weight, (with_cos[1] + with_sin[0]) * weight],
        axis=1,
    )


def solution(mesh):
    blk, wide = mesh.shape["blk"], mesh.shape["wide"]

    def on_device(coupling, rp_cells, re_cells, q_points, k_points, mode_energy):
        args = (coupling, rp_cells, re_cells, q_points, k_points, mode_energy)
        slab, cells, _, total = coupling.shape
        waves = k_points.shape[1]
        fits = (
            blk == 8
            and total // wide == LANES
            and cells == 2
            and wide == 4
            and waves == 2
            and slab % 128 == 0
            and q_points.shape[1] % LANES == 0
        )
        if not fits:
            return general(*args)
        return direct(blk, wide, *args)

    in_specs = (
        P("blk", "wide", None, None),
        P(),
        P(None, "wide"),
        P(None, "blk"),
        P(),
        P(None, "blk"),
    )
    out_specs = P(None, None, "wide", "blk")
    return jax.shard_map(
        on_device, mesh=mesh, in_specs=in_specs, out_specs=out_specs, check_vma=False
    )
```

```python
import functools
import math

import jax
import jax.numpy as jnp
from jax import lax
from jax.experimental import pallas as pl
from jax.experimental.pallas import tpu as pltpu
from jax.sharding import PartitionSpec as P


MODES = 16
MESHQ = 32
MESHK = 32
LANES = 128
TAIL = 2
NEAR = (6, 4, 2)
LAST = 96
ORDER = ("pair", "two", "three", "one", "sum")
EARLY = 0
CODED = 1
BITS = 14.0


def xor_pairs(count, step):
    return [(i, i ^ step) for i in range(count)]


def swap(value, axis, count, step):
    return lax.ppermute(value, axis, xor_pairs(count, step))


def grant(mebibytes):
    return pltpu.CompilerParams(vmem_limit_bytes=int(mebibytes * 2**20))


def cut_kernel(parts, rings, more, entries, x_ref, cells_ref, points_ref, *rest):
    extra, rest = rest[:more], rest[more:]
    outs = rest[: len(parts)]
    cells, points, sem, small = rest[-4:]
    me = lax.axis_index("wide")
    copies = [
        pltpu.make_async_copy(cells_ref, cells, small.at[0]),
        pltpu.make_async_copy(points_ref, points, small.at[1]),
    ]
    for i, (step, first, rows) in enumerate(parts):
        column = pl.multiple_of((me ^ step) * entries, LANES)
        copies.append(
            pltpu.make_async_copy(
                x_ref.at[pl.ds(first, rows), :, :, pl.ds(column, entries)],
                outs[i].at[pl.ds(0, rows)],
                sem.at[i],
            )
        )
    for i in range(more):
        out = rest[len(parts) + 2 * rings + i]
        copies.append(pltpu.make_async_copy(extra[i], out, small.at[2 + i]))
    for copy in copies:
        copy.start()
    if rings:
        rest[len(parts)][...], rest[len(parts) + 1][...] = circle(MESHK)
    for copy in copies[:2]:
        copy.wait()
    shape = (TAIL,) + outs[0].shape[1:]
    which_cell = lax.broadcasted_iota(jnp.int32, shape, 1)
    which_wave = lax.broadcasted_iota(jnp.int32, shape, 2)
    tail = jnp.zeros(shape, jnp.float32)
    for r in range(cells.shape[0]):
        for k in range(points.shape[0]):
            turn = cells[r, 0] * points[k, 0]
            for axis in range(1, cells.shape[1]):
                turn += cells[r, axis] * points[k, axis]
            turn = lax.rem(lax.rem(turn, MESHK) + MESHK, MESHK)
            here = (which_cell == r) & (which_wave == k)
            tail = jnp.where(here, turn.astype(jnp.float32), tail)
    tail = tail.astype(outs[0].dtype)
    for (_, _, rows), out in zip(parts, outs):
        out[pl.ds(rows, TAIL)] = tail
    for copy in copies[2:]:
        copy.wait()


def stay(array):
    return pltpu.with_memory_space_constraint(array, pltpu.HBM)


def cut(coupling, re_cells, k_points, parts, rings, extra, entries):
    cells = coupling.shape[1]
    shapes = [
        jax.ShapeDtypeStruct((rows + TAIL, cells, 2, entries), coupling.dtype)
        for _, _, rows in parts
    ]
    count = len(shapes)
    shapes += [jax.ShapeDtypeStruct((8, LANES), jnp.float32)] * (2 * rings)
    shapes += [jax.ShapeDtypeStruct(array.shape, array.dtype) for array in extra]
    arrays = (coupling, re_cells.T, k_points.T) + tuple(extra)
    outs = pl.pallas_call(
        functools.partial(cut_kernel, parts, rings, len(extra), entries),
        out_shape=shapes,
        in_specs=[pl.BlockSpec(memory_space=pltpu.HBM)] * len(arrays),
        out_specs=[pl.BlockSpec(memory_space=pltpu.VMEM)] * len(shapes),
        scratch_shapes=[
            pltpu.SMEM(re_cells.shape[::-1], jnp.int32),
            pltpu.SMEM(k_points.shape[::-1], jnp.int32),
            pltpu.SemaphoreType.DMA((count,)),
            pltpu.SemaphoreType.DMA((2 + len(extra),)),
        ],
        compiler_params=grant(2),
        name="cut",
    )(*[stay(array) for array in arrays])
    return outs[:count], outs[count:]


def circle(modulus):
    lane = lax.broadcasted_iota(jnp.int32, (8, LANES), 1) % modulus
    angle = lane.astype(jnp.float32) * (2.0 * math.pi / modulus)
    return jnp.cos(angle), jnp.sin(angle)


def look(values, index):
    return jnp.take_along_axis(values, index, axis=1, mode="promise_in_bounds")


def combine_kernel(spans, rows, cells, waves, adds, cos_ref, sin_ref, *refs):
    count = len(spans)
    ins, plus = refs[:count], refs[count : count + len(adds)]
    out, work, sums = refs[-3:]
    entries = work.shape[2]
    coded = out.dtype == jnp.int16
    target = sums if coded else out
    per = 2 * cells
    phases = []
    for i, ref in enumerate(ins):
        work[i, pl.ds(0, ref.shape[0]), :] = ref[...].astype(jnp.float32)
    for i, (_, size) in enumerate(spans):
        turn = work[i, pl.ds(size * per, 8), :].astype(jnp.int32)
        phases.append((look(cos_ref[...], turn), look(sin_ref[...], turn)))
    step = 32
    for first in range(0, rows, step):
        re = [None] * waves
        im = [None] * waves
        for (begin, size), ref in zip(adds, plus):
            if not begin <= first < begin + size:
                continue
            for k in range(waves):
                lanes = pl.ds(k * entries, entries)
                x = ref[pl.ds(first - begin, step), lanes].astype(jnp.float32)
                y = ref[pl.ds(size + first - begin, step), lanes].astype(jnp.float32)
                if ref.dtype == jnp.int16:
                    power = ref[pl.ds(2 * size, 16), lanes].astype(jnp.float32)
                    unit = jnp.exp2(power[0:1, :] - BITS)
                    x, y = x * unit, y * unit
                re[k] = x if re[k] is None else re[k] + x
                im[k] = y if im[k] is None else im[k] + y
        for i, (begin, size) in enumerate(spans):
            if not begin <= first < begin + size:
                continue
            cos, sin = phases[i]
            for r in range(cells):
                start = (first - begin) * per + 2 * r
                a = work[i, pl.ds(start, step, stride=per), :]
                b = work[i, pl.ds(start + 1, step, stride=per), :]
                for k in range(waves):
                    at = r * waves + k
                    c = cos[at : at + 1, :]
                    s = sin[at : at + 1, :]
                    x = c * a - s * b
                    y = c * b + s * a
                    re[k] = x if re[k] is None else re[k] + x
                    im[k] = y if im[k] is None else im[k] + y
        for k in range(waves):
            lanes = pl.ds(k * entries, entries)
            target[pl.ds(first, step), lanes] = re[k].astype(target.dtype)
            target[pl.ds(rows + first, step), lanes] = im[k].astype(target.dtype)
    if coded:
        value = sums[...]
        top = jnp.max(jnp.abs(value), axis=0, keepdims=True)
        power = jnp.ceil(jnp.log2(jnp.maximum(top, 2.0**-100)))
        scaled = jnp.round(value * jnp.exp2(BITS - power)).astype(jnp.int32)
        out[pl.ds(0, 2 * rows), :] = scaled.astype(jnp.int16)
        spread = jnp.broadcast_to(power, (16, value.shape[1])).astype(jnp.int32)
        out[pl.ds(2 * rows, 16), :] = spread.astype(jnp.int16)


def combine(circles, blocks, spans, plus, adds, rows, waves, dtype):
    cells, _, entries = blocks[0].shape[1:]
    flat = [b.reshape(b.shape[0] * 2 * cells, entries) for b in blocks]
    full = max(b.shape[0] for b in flat)
    coded = dtype == jnp.int16
    shape = (2 * rows, waves * entries)
    tall = (2 * rows + 16 * coded, waves * entries)
    return pl.pallas_call(
        functools.partial(combine_kernel, spans, rows, cells, waves, adds),
        out_shape=jax.ShapeDtypeStruct(tall, dtype),
        in_specs=[pl.BlockSpec(memory_space=pltpu.VMEM)] * (2 + len(flat) + len(plus)),
        out_specs=pl.BlockSpec(memory_space=pltpu.VMEM),
        scratch_shapes=[
            pltpu.VMEM((len(flat), full, entries), jnp.float32),
            pltpu.VMEM(shape if coded else (8, LANES), jnp.float32),
        ],
        compiler_params=grant(6),
        name="combine",
    )(*circles, *flat, *plus)


def table_kernel(slab, rp_ref, q_ref, out_ref):
    cos_table, sin_table = circle(MESHQ)
    blocks = out_ref.shape[0]
    q_local = q_ref.shape[1]
    step = 32
    q = q_ref[...].astype(jnp.bfloat16)
    for block in range(blocks):
        n = lax.dot_general(
            rp_ref[:, pl.ds(block * slab, slab)].astype(jnp.bfloat16),
            q,
            (((0,), (0,)), ((), ())),
            preferred_element_type=jnp.float32,
        )
        m = n - MESHQ * jnp.floor(n * (1.0 / MESHQ))
        index = m.astype(jnp.int32)
        for top in range(0, slab, step):
            for left in range(0, q_local, LANES):
                cos_rows = []
                sin_rows = []
                for sub in range(top, top + step, 8):
                    at = index[sub : sub + 8, left : left + LANES]
                    cos_rows.append(look(cos_table, at))
                    sin_rows.append(look(sin_table, at))
                c = jnp.concatenate(cos_rows, axis=0).astype(jnp.bfloat16)
                s = jnp.concatenate(sin_rows, axis=0).astype(jnp.bfloat16)
                near = pl.ds(left, LANES)
                far = pl.ds(q_local + left, LANES)
                out_ref[block, pl.ds(top, step), near] = c
                out_ref[block, pl.ds(top, step), far] = s
                out_ref[block, pl.ds(slab + top, step), near] = -s
                out_ref[block, pl.ds(slab + top, step), far] = c


def table(rp_cells, q_points, slab):
    blocks = rp_cells.shape[1] // slab
    q_local = q_points.shape[1]
    shape = (blocks, 2 * slab, 2 * q_local)
    return pl.pallas_call(
        functools.partial(table_kernel, slab),
        out_shape=jax.ShapeDtypeStruct(shape, jnp.bfloat16),
        in_specs=[pl.BlockSpec(memory_space=pltpu.VMEM)] * 2,
        out_specs=pl.BlockSpec(memory_space=pltpu.VMEM),
        compiler_params=grant(6),
        cost_estimate=pl.CostEstimate(
            flops=8 * blocks * slab * q_local * 10,
            bytes_accessed=blocks * slab * q_local * 8,
            transcendentals=0,
        ),
        name="table",
    )(rp_cells, q_points)


def partial_kernel(pieces, more, table_ref, *refs):
    ins, out = refs[:-1], refs[-1]
    me = lax.axis_index("blk")
    total = ins[-1][...] if more else None
    for i, step in enumerate(pieces):
        part = lax.dot_general(
            ins[i][...],
            table_ref[me ^ step],
            (((0,), (0,)), ((), ())),
            preferred_element_type=jnp.float32,
        )
        total = part if total is None else total + part
    out[...] = total


def partial(tables, held, total):
    blocks = [value for value, _ in held]
    pieces = [piece for _, piece in held]
    shape = (blocks[0].shape[1], tables.shape[2])
    depth = len(pieces) * tables.shape[1]
    more = [] if total is None else [total]
    return pl.pallas_call(
        functools.partial(partial_kernel, pieces, bool(more)),
        out_shape=jax.ShapeDtypeStruct(shape, jnp.float32),
        in_specs=[pl.BlockSpec(memory_space=pltpu.VMEM)] * (1 + len(blocks) + len(more)),
        out_specs=pl.BlockSpec(memory_space=pltpu.VMEM),
        compiler_params=grant(8),
        cost_estimate=pl.CostEstimate(
            flops=2 * depth * shape[0] * shape[1],
            bytes_accessed=4 * shape[0] * shape[1],
            transcendentals=0,
        ),
        name="partial",
    )(tables, *blocks, *more)


def finish_kernel(pieces, waves, entries, table_ref, energy_ref, sum_ref, *refs):
    ins, out, held, sem = refs[:-3], refs[-3], refs[-2], refs[-1]
    me = lax.axis_index("blk")
    q_local = energy_ref.shape[1]
    weight = 1.0 / jnp.sqrt(2.0 * energy_ref[...])
    copies = []
    for k in range(waves):
        lanes = pl.ds(k * entries, entries)
        total = sum_ref[lanes, :]
        for i, step in enumerate(pieces):
            total += lax.dot_general(
                ins[i][:, lanes],
                table_ref[me ^ step],
                (((0,), (0,)), ((), ())),
                preferred_element_type=jnp.float32,
            )
        for part in range(2):
            for e in range(0, entries, MODES):
                held[k, part, pl.ds(e, MODES), :] = (
                    total[e : e + MODES, part * q_local : (part + 1) * q_local] * weight
                )
        copies.append(pltpu.make_async_copy(held.at[k], out.at[k], sem.at[k]))
        copies[-1].start()
    for copy in copies:
        copy.wait()


def finish(tables, energy, total, blocks, pieces, waves, entries):
    q_local = energy.shape[1]
    shape = (waves, 2, entries, q_local)
    return pl.pallas_call(
        functools.partial(finish_kernel, pieces, waves, entries),
        out_shape=jax.ShapeDtypeStruct(shape, jnp.float32),
        in_specs=[pl.BlockSpec(memory_space=pltpu.VMEM)] * (3 + len(blocks)),
        out_specs=pl.BlockSpec(memory_space=pl.ANY),
        scratch_shapes=[
            pltpu.VMEM(shape, jnp.float32),
            pltpu.SemaphoreType.DMA((waves,)),
        ],
        compiler_params=grant(8),
        name="finish",
    )(tables, energy, total, *blocks)


def direct(blk, wide, coupling, rp_cells, re_cells, q_points, k_points, mode_energy):
    slab, _, _, total = coupling.shape
    entries = total // wide
    waves = k_points.shape[1]
    most = slab - LAST
    rest = (most, LAST)

    sent = {"one": (1, 0, slab), "two": (2, 0, most), "three": (3, 0, most)}
    if LAST:
        sent["pair"] = (3, most, LAST)
    if not most:
        del sent["two"], sent["three"]
    names = [name for name in ORDER if name in sent]
    parts = [sent[name] for name in names] + [(2, most, LAST)] * bool(LAST)
    arrays = (coupling, re_cells, k_points)
    cuts, circles = cut(*arrays, parts, True, [], entries)
    mid = list(cuts[len(names) :])
    extra = (rp_cells, q_points)
    (own,), extra = cut(*arrays, [(0, 0, slab)], False, extra, entries)
    tables = table(*extra, slab)

    got = {}
    for name, block in zip(names, cuts):
        got[name] = swap(block, "wide", wide, 1 if name == "pair" else sent[name][0])
    plus, adds = [], []
    if LAST:
        dtype = jnp.int16 if CODED else jnp.bfloat16
        both = combine(
            circles, mid + [got["pair"]], [(0, LAST)] * 2, [], [], LAST, waves, dtype
        )
        plus.append(swap(both, "wide", wide, 2))
        adds.append(rest)
    blocks, spans = [own, got["one"]], [(0, slab)] * 2
    if EARLY:
        some = combine(circles, blocks, spans, [], [], slab, waves, jnp.float32)
        plus.append(some)
        adds.append((0, slab))
        blocks, spans = [], []
    if most:
        blocks += [got["two"], got["three"]]
        spans += [(0, most)] * 2
    mine = combine(circles, blocks, spans, plus, adds, slab, waves, jnp.bfloat16)

    held = {0: mine}
    for step in range(blk - 2, 0, -2):
        held[step] = swap(mine, "blk", blk, step)
    for step in list(held):
        held[step + 1] = swap(held[step], "blk", blk, 1)
    first, second, third = NEAR
    groups = [
        (0, 1, first),
        (third, first + 1, second),
        (third + 1, second + 1),
    ]
    total = None
    for steps in groups[:-1]:
        total = partial(tables, [(held[step], step) for step in steps], total)
    return finish(
        tables,
        mode_energy,
        total,
        [held[step] for step in groups[-1]],
        groups[-1],
        waves,
        entries,
    )


def phase_parts(left, right, modulus):
    whole = jnp.sum(left[:, :, None] * right[:, None, :], axis=0)
    angle = jnp.mod(whole, modulus).astype(jnp.float32) * (2.0 * math.pi / modulus)
    return (jnp.cos(angle), jnp.sin(angle))


def general(coupling, rp_cells, re_cells, q_points, k_points, mode_energy):
    moved = lax.all_to_all(coupling, "wide", split_axis=3, concat_axis=1, tiled=True)
    cells = lax.all_gather(re_cells, "wide", axis=1, tiled=True)
    entries = moved.shape[3]
    offset = lax.axis_index("wide") * entries
    k_cos, k_sin = phase_parts(k_points, cells, MESHK)
    real = moved[:, :, 0].astype(jnp.float32)
    imag = moved[:, :, 1].astype(jnp.float32)
    high = lax.Precision.HIGHEST
    turn = functools.partial(jnp.einsum, "kr,pre->pke", precision=high)
    held = jnp.stack(
        [turn(k_cos, real) - turn(k_sin, imag), turn(k_cos, imag) + turn(k_sin, real)],
        axis=2,
    ).astype(coupling.dtype)
    full = lax.all_gather(held, "blk", axis=0, tiled=True)
    cosine, sine = phase_parts(q_points, rp_cells, MESHQ)
    dot = functools.partial(
        jnp.einsum, "qp,pkse->skeq", preferred_element_type=jnp.float32
    )
    with_cos = dot(cosine.astype(full.dtype), full)
    with_sin = dot(sine.astype(full.dtype), full)
    index = (offset + jnp.arange(entries, dtype=jnp.int32)) % MODES
    weight = (1.0 / jnp.sqrt(2.0 * mode_energy))[index]
    return jnp.stack(
        [(with_cos[0] - with_sin[1]) * weight, (with_cos[1] + with_sin[0]) * weight],
        axis=1,
    )


def solution(mesh):
    blk, wide = mesh.shape["blk"], mesh.shape["wide"]

    def on_device(coupling, rp_cells, re_cells, q_points, k_points, mode_energy):
        args = (coupling, rp_cells, re_cells, q_points, k_points, mode_energy)
        slab, cells, _, total = coupling.shape
        waves = k_points.shape[1]
        fits = (
            blk == 8
            and total // wide == LANES
            and cells == 2
            and wide == 4
            and waves == 2
            and slab % 128 == 0
            and q_points.shape[1] % LANES == 0
        )
        if not fits:
            return general(*args)
        return direct(blk, wide, *args)

    in_specs = (
        P("blk", "wide", None, None),
        P(),
        P(None, "wide"),
        P(None, "blk"),
        P(),
        P(None, "blk"),
    )
    out_specs = P(None, None, "wide", "blk")
    return jax.shard_map(
        on_device, mesh=mesh, in_specs=in_specs, out_specs=out_specs, check_vma=False
    )
```
